32 devices in a mesh: seq: 8 (over z, core), tp: 4 (over y, x).
Axes of the slice: x: 2, y: 2, z: 4, core: 2. Of those that a mesh axis runs over, the one named last changes fastest.
Arguments:
- streams: bfloat16 [4096, 4, 4096], P('seq', None, 'tp'), may hold values from -6 to 6
- doc_ids: int32 [4096], P('seq'), may hold values from 0 to 3, never falling along the last dimension, each value on 1 to 2048 neighbouring positions
- mix_weight: float32 [4, 4096, 24], P(None, 'tp'), may hold values from -0.046875 to 0.046875
- mix_bias: float32 [24], replicated, may hold values from -1 to 1
- attn_gain: float32 [4096], replicated, may hold values from 0.1 to 1.9
- w_qkv: bfloat16 [4096, 3, 4096], P(None, None, 'tp'), may hold values from -1 to 1
- w_out: bfloat16 [4096, 4096], P('tp'), may hold values from -0.5 to 0.5
Outputs:
- new_streams: bfloat16 [4096, 4, 4096], P('seq', None, 'tp')
The draws below stay inside these ranges and needn't reach their ends.
Inputs may be any that keep to these rules, and one draw needn't show every extreme that they name: doc_ids never fall along the sequence; each of the 4 documents has 1 to 2048 positions, and the longest has exactly 2048.
All inputs are finite; a program needn't handle non-finite values.
Results may differ from the reference program's by a relative error of at most 0.014.
The reference program's roundings to bfloat16 on the way count: a program that leaves them out, or rounds other values in their place, can miss the bound.
Values may be sent and summed in bfloat16 or wider, within the bound.
No kernel may reach another device: no remote copies, remote signals or barrier semaphores. Data moves between devices by JAX's collectives and lax.ppermute only.
A program may use at most 256 MiB of HBM per device.

```python
import math
import jax
import jax.numpy as jnp
import numpy as np
from jax import lax

D = 4096
HEADS = 32
HEAD_DIM = 128
STREAMS = 4
BALANCE_ROUNDS = 20
DOCS = 4
TOKENS = 4096
COEFS = 24


def draw_w_qkv(key, part):
    key_base = jax.random.fold_in(key, 11)
    scale_in = jnp.float32(D) ** (-0.5)
    base = jax.random.normal(key_base, (D, 3, D), jnp.float32) * scale_in
    base = jnp.clip(base, -4.0 * scale_in, 4.0 * scale_in)
    return base.astype(jnp.bfloat16)


def block_scale(stream_key, extent, cuts, least, high):
    gain, own = 1.0, jax.random.fold_in(stream_key, 6)
    for position, shards_of in cuts:
        steps = jnp.exp(jax.random.uniform(jax.random.fold_in(own, position), (shards_of,), jnp.float32, least / len(cuts), high / len(cuts)))
        gain = gain * jnp.repeat(steps, extent[position] // shards_of).reshape([-1 if axis == position else 1 for axis in range(len(extent))])
    return gain


def length_profile(number_of, total, most, skew):
    loads = [(1 << 20) // math.isqrt(grade ** skew) + 1 for grade in range(2, number_of + 1)]
    spare, counts = total - most - (number_of - 1), [1] * (number_of - 1)
    while spare > 0:
        free = [i for i in range(number_of - 1) if counts[i] < most]
        whole, left = sum([loads[i] for i in free]), spare
        for i in free:
            more = min(most - counts[i], max(1, left * loads[i] // whole), spare)
            counts[i] = counts[i] + more
            spare = spare - more
    return np.array([most] + counts)


def uneven_parts(stream_key, number_of, total, limit, slope):
    if number_of == 2:
        one = jax.random.randint(stream_key, (), max(1, total - limit), min(limit, total - 1) + 1)
        return jnp.stack([one, total - one])
    sizes = jnp.asarray(length_profile(number_of, total, limit, slope), jnp.int32)
    twos = (number_of - 1) // 2
    source_of, taker = sizes[1:1 + 2 * twos:2], sizes[2:2 + 2 * twos:2]
    margin = jnp.minimum(source_of - 1, limit - taker)
    passed = jax.random.randint(jax.random.fold_in(stream_key, 1), (twos,), 0, 1 << 20) % (margin + 1)
    sizes = sizes.at[1:1 + 2 * twos:2].set(source_of - passed).at[2:2 + 2 * twos:2].set(taker + passed)
    return sizes[jax.random.permutation(jax.random.fold_in(stream_key, 2), number_of)]


def scatter_about(key, shape, width, limit, pieces=(), held_as=jnp.bfloat16):
    loudness = block_scale(key, shape, pieces, -0.22, 0.18) if pieces else 1.0
    result = jax.random.normal(key, shape, jnp.float32) * width * loudness
    return jnp.minimum(jnp.maximum(result, -limit), limit).astype(held_as)


def setup_inputs(seed: int = 0) -> dict:
    key_list = jax.random.split(jax.random.key(seed), 8)
    return {
        "streams": scatter_about(key_list[0], (TOKENS, STREAMS, D), 1.0, 6.0, ((0, 8), (2, 4))),
        "doc_ids": jnp.searchsorted(jnp.cumsum(uneven_parts(key_list[1], DOCS, TOKENS, TOKENS // 2, 0)), jnp.arange(TOKENS), side="right").astype(jnp.int32),
        "mix_weight": scatter_about(key_list[2], (STREAMS, D, COEFS), (STREAMS * D) ** -0.5, 0.046875, ((1, 4),), jnp.float32),
        "mix_bias": jnp.clip(jax.random.uniform(key_list[3], (COEFS,), jnp.float32, -1.0, 1.0), -1.0, 1.0),
        "attn_gain": jnp.clip(1.0 + 0.18 * jax.random.normal(key_list[4], (D,), jnp.float32), 0.1, 1.9),
        "w_qkv": draw_w_qkv(jax.random.fold_in(key_list[7], 71), 0),
        "w_out": scatter_about(key_list[6], (D, D), HEAD_DIM ** -0.5, 0.5, ((0, 4),)),
    }


masked_score = -1e+30
norm_eps = 1e-06

def doubly_stochastic(mixing_matrix):

    def balance_round(round_index, running_matrix):
        running_matrix = running_matrix / lax.optimization_barrier(jnp.sum(running_matrix, axis=2, keepdims=True))
        return running_matrix / lax.optimization_barrier(jnp.sum(running_matrix, axis=1, keepdims=True))
    return lax.fori_loop(0, BALANCE_ROUNDS, balance_round, mixing_matrix)

def coefficients(squares, partial_logits, mix_bias):
    root_mean = jnp.sqrt(squares / (STREAMS * D) + norm_eps)
    coef_logits = partial_logits / root_mean[:, None] + mix_bias
    input_weights = jax.nn.sigmoid(coef_logits[:, :STREAMS])
    output_weights = 2.0 * jax.nn.sigmoid(coef_logits[:, STREAMS:2 * STREAMS])
    unnormalized_mixing = jnp.exp(coef_logits[:, 2 * STREAMS:]).reshape(-1, STREAMS, STREAMS)
    return (input_weights, output_weights, doubly_stochastic(unnormalized_mixing))

def head_attention(queries, keys, values, doc_ids):
    positions = jnp.arange(TOKENS, dtype=jnp.int32)
    block_rows = math.gcd(512, TOKENS)

    def one_block(first_row):
        query_block = lax.dynamic_slice_in_dim(queries, first_row, block_rows, 0)
        query_pos = first_row + jnp.arange(block_rows, dtype=jnp.int32)
        query_doc = lax.dynamic_slice_in_dim(doc_ids, first_row, block_rows, 0)
        scores = jnp.dot(query_block, keys.T, preferred_element_type=jnp.float32) * HEAD_DIM ** (-0.5)
        allowed = (positions[None, :] <= query_pos[:, None]) & (doc_ids[None, :] == query_doc[:, None])
        scores = jnp.where(allowed, scores, masked_score)
        row_max = lax.optimization_barrier(jnp.max(scores, axis=1, keepdims=True))
        exp_weights = jnp.where(allowed, jnp.exp(scores - row_max), 0.0)
        numerator = jnp.dot(exp_weights.astype(jnp.bfloat16), values, preferred_element_type=jnp.float32)
        return (numerator / lax.optimization_barrier(jnp.sum(exp_weights, axis=1, keepdims=True))).astype(jnp.bfloat16)
    block_starts = jnp.arange(TOKENS // block_rows, dtype=jnp.int32) * block_rows
    return lax.map(one_block, block_starts).reshape(TOKENS, HEAD_DIM)

def reference(streams, doc_ids, mix_weight, mix_bias, attn_gain, w_qkv, w_out):
    wide_streams = streams.astype(jnp.float32)
    squares = lax.optimization_barrier(jnp.sum(wide_streams * wide_streams, axis=(1, 2)))
    partial_logits = jnp.einsum('tsd,sdc->tc', wide_streams, mix_weight, precision=lax.Precision.HIGHEST)
    input_weights, output_weights, mixing = coefficients(squares, partial_logits, mix_bias)
    mixed_input = jnp.einsum('ts,tsd->td', input_weights, wide_streams, precision=lax.Precision.HIGHEST).astype(jnp.bfloat16)
    input_wide = mixed_input.astype(jnp.float32)
    norm_scale = lax.rsqrt(lax.optimization_barrier(jnp.mean(input_wide * input_wide, axis=1)) + norm_eps)
    gained = (input_wide * attn_gain).astype(jnp.bfloat16)
    projected = jnp.dot(gained, w_qkv.reshape(D, 3 * D), preferred_element_type=jnp.float32)
    projected = (projected * norm_scale[:, None]).astype(jnp.bfloat16).reshape(TOKENS, 3, HEADS, HEAD_DIM)
    per_head = jnp.moveaxis(projected, 2, 0)
    context = lax.map(lambda head_slab: head_attention(head_slab[:, 0], head_slab[:, 1], head_slab[:, 2], doc_ids), per_head)
    context = jnp.moveaxis(context, 0, 1).reshape(TOKENS, D)
    branch_out = jnp.dot(context, w_out, preferred_element_type=jnp.float32)
    carried = jnp.einsum('tij,tjd->tid', mixing, wide_streams, precision=lax.Precision.HIGHEST)
    return (carried + output_weights[:, :, None] * branch_out[:, None, :]).astype(jnp.bfloat16)
```

```python
import functools

import jax
import jax.numpy as jnp
from jax import lax
from jax.experimental import pallas as pl
from jax.experimental.pallas import tpu as pltpu
from jax.sharding import PartitionSpec as P

HEAD_DIM = 128
BALANCE_ROUNDS = 20
DOCS = 4
GATHER_CHUNKS = 4
SCATTER_CHUNKS = 2

masked_score = -1e30
norm_eps = 1e-06
VMEM_LIMIT = 60 * 1024 * 1024


bf16 = jnp.bfloat16
f32 = jnp.float32


def by_xor(value, axis, bit):
    count = lax.axis_size(axis)
    return lax.ppermute(value, axis, [(i, i ^ bit) for i in range(count)])


def next_chip(value):
    count = lax.axis_size("seq")
    return lax.ppermute(value, "seq", [(i, i + 2) for i in range(count - 2)])


def gathered_ids(doc_ids):
    count = lax.axis_size("seq")
    index = lax.axis_index("seq")
    held, bit = doc_ids, 1
    while bit < count:
        other = by_xor(held, "seq", bit)
        mine_first = (index & bit) == 0
        held = jnp.concatenate(
            [jnp.where(mine_first, held, other), jnp.where(mine_first, other, held)]
        )
        bit *= 2
    return held


def tp_sum(value):
    count = lax.axis_size("tp")
    if count == 4:
        return (value + by_xor(value, "tp", 1)) + (by_xor(value, "tp", 2) + by_xor(value, "tp", 3))
    return lax.psum(value, "tp")


def doubly_stochastic(mixing):
    side = len(mixing)
    grid = jnp.stack([jnp.stack(row) for row in mixing])

    def balance_round(_, running):
        running = running / jnp.sum(running, axis=1, keepdims=True)
        return running / jnp.sum(running, axis=0, keepdims=True)

    return lax.fori_loop(0, BALANCE_ROUNDS, balance_round, grid)


def project_kernel(ids, own, rem, o_own, o_rem, gain, w, q_in, q_out, kv_out, gained, scale, *, pieces, m, width):
    step = pl.program_id(0)
    half = pl.program_id(1)

    @pl.when((step == 0) & (half == 0))
    def _():
        for side, (first, rest) in enumerate(((own, rem), (o_own, o_rem))):
            total = jnp.zeros((m, 1), f32)
            for k in range(pieces):
                x = first[...] if k == 0 else rest[(k - 1) * m : k * m, :]
                x = x.astype(f32)
                total = total + jnp.sum(x * x, axis=1, keepdims=True)
                g = gain[pl.ds(ids[k], 1), :]
                gained[side * m : (side + 1) * m, k * width : (k + 1) * width] = (x * g).astype(bf16)
            scale[side * m : (side + 1) * m, :] = jnp.broadcast_to(
                lax.rsqrt(total / (pieces * width) + norm_eps), (m, 128)
            )

    acc = None
    for k in range(pieces):
        row = pl.multiple_of(ids[k] * width, width)
        part = jnp.dot(
            gained[:, k * width : (k + 1) * width],
            w[0, pl.ds(row, width), :],
            preferred_element_type=f32,
        )
        acc = part if acc is None else acc + part
    result = (acc * scale[:, 0:1]).astype(bf16)

    @pl.when(step == 2)
    def _():
        q_out[...] = result

    @pl.when(step < 2)
    def _():
        kv_out[0] = result


def project(ids, core, own, rem, o_own, o_rem, gain, w3, q_full, chunk):
    m, width = own.shape
    pieces = rem.shape[0] // m + 1
    local_width = w3.shape[2] // 2
    tile = min(256, local_width)
    tiles = local_width // tile
    scalars = jnp.concatenate([ids, core[None]]).astype(jnp.int32)
    n_ids = pieces

    def w_map(step, half, s):
        return ((step + 1) % 3, 0, s[n_ids] * tiles + half)

    full = lambda a: pl.BlockSpec(a.shape, lambda step, half, s: (0,) * a.ndim)
    grid_spec = pltpu.PrefetchScalarGridSpec(
        num_scalar_prefetch=1,
        grid=(3, tiles),
        in_specs=[
            full(own), full(rem), full(o_own), full(o_rem), full(gain),
            pl.BlockSpec((1, pieces * width, tile), w_map),
            pl.BlockSpec(memory_space=pl.ANY),
        ],
        out_specs=[
            pl.BlockSpec((2 * m, tile), lambda step, half, s: (chunk, jnp.where(step == 2, half, 0))),
            pl.BlockSpec(
                (1, 2 * m, tile),
                lambda step, half, s: (jnp.minimum(step, 1), 0, jnp.where(step < 2, half, tiles - 1)),
            ),
        ],
        scratch_shapes=[
            pltpu.VMEM((2 * m, pieces * width), bf16),
            pltpu.VMEM((2 * m, 128), f32),
        ],
    )
    return pl.pallas_call(
        functools.partial(project_kernel, pieces=pieces, m=m, width=width),
        grid_spec=grid_spec,
        out_shape=[
            jax.ShapeDtypeStruct(q_full.shape, bf16),
            jax.ShapeDtypeStruct((2, 2 * m, local_width), bf16),
        ],
        input_output_aliases={7: 0},
        compiler_params=pltpu.CompilerParams(vmem_limit_bytes=VMEM_LIMIT),
        cost_estimate=pl.CostEstimate(
            flops=2 * 2 * m * pieces * width * 3 * local_width,
            bytes_accessed=pieces * width * 3 * local_width * 2,
            transcendentals=0,
        ),
        name=f"project{chunk}",
    )(scalars, own, rem, o_own, o_rem, gain, w3, q_full)


def attend_kernel(q, start, pos, kpos, *refs, count, first, final, m):
    kvs = refs[:count]
    refs = refs[count:]
    if not first:
        ml_in, acc_in = refs[:2]
        refs = refs[2:]
    queries = q[...]
    begin = start[...]
    factor = HEAD_DIM**-0.5
    scores, offset = [], 0
    for kv in kvs:
        keys = kv.shape[1]
        s = lax.dot_general(
            queries, kv[0], (((1,), (1,)), ((), ())), preferred_element_type=f32
        )
        where = kpos[:, offset : offset + keys]
        allowed = where >= begin
        if first:
            allowed = allowed & (where <= pos[...])
        scores.append(jnp.where(allowed, s * factor, masked_score))
        offset += keys
    top = functools.reduce(jnp.maximum, [jnp.max(s, axis=1, keepdims=True) for s in scores])
    if not first:
        old_top, old_sum = ml_in[0][:, 0:1], ml_in[0][:, 1:2]
        top = jnp.maximum(top, old_top)
    total, acc = None, None
    for s, kv in zip(scores, kvs):
        p = jnp.exp(s - top)
        row = jnp.sum(p, axis=1, keepdims=True)
        part = jnp.dot(p.astype(bf16), kv[1], preferred_element_type=f32)
        total = row if total is None else total + row
        acc = part if acc is None else acc + part
    if not first:
        rescale = jnp.exp(old_top - top)
        total = total + old_sum * rescale
        acc = acc + acc_in[0] * rescale
    if final:
        keep, send = refs
        context = (acc / total).astype(bf16)
        keep[...] = context[:m]
        send[...] = context[m:]
    else:
        ml_out, acc_out = refs
        lane = lax.broadcasted_iota(jnp.int32, (queries.shape[0], 128), 1)
        ml_out[0] = jnp.where(lane == 0, top, total)
        acc_out[0] = acc


def attend(q, start, pos, kpos, kvs, state, m, final, name):
    rows, width = q.shape
    heads = width // HEAD_DIM
    block = 2 * m
    first = state is None
    keys = sum(kv.shape[1] for kv in kvs)
    in_specs = [
        pl.BlockSpec((block, HEAD_DIM), lambda h, i: (i, h)),
        pl.BlockSpec((block, 1), lambda h, i: (i, 0)),
        pl.BlockSpec((block, 1), lambda h, i: (i, 0)),
        pl.BlockSpec((1, keys), lambda h, i: (0, 0)),
    ]
    in_specs += [pl.BlockSpec((2, kv.shape[1], HEAD_DIM), lambda h, i: (0, 0, h)) for kv in kvs]
    operands = [q, start, pos, kpos, *kvs]
    state_specs = [
        pl.BlockSpec((1, block, 128), lambda h, i: (h, i, 0)),
        pl.BlockSpec((1, block, HEAD_DIM), lambda h, i: (h, i, 0)),
    ]
    aliases = {}
    if not first:
        if not final:
            aliases = {len(operands): 0, len(operands) + 1: 1}
        operands += list(state)
        in_specs += state_specs
    if final:
        out_specs = [pl.BlockSpec((m, HEAD_DIM), lambda h, i: (i, h))] * 2
        out_shape = [jax.ShapeDtypeStruct((rows // 2, width), bf16)] * 2
    else:
        out_specs = state_specs
        out_shape = [
            jax.ShapeDtypeStruct((heads, rows, 128), f32),
            jax.ShapeDtypeStruct((heads, rows, HEAD_DIM), f32),
        ]
    return pl.pallas_call(
        functools.partial(attend_kernel, count=len(kvs), first=first, final=final, m=m),
        grid=(heads, rows // block),
        in_specs=in_specs,
        out_specs=out_specs,
        out_shape=out_shape,
        input_output_aliases=aliases,
        compiler_params=pltpu.CompilerParams(vmem_limit_bytes=VMEM_LIMIT),
        cost_estimate=pl.CostEstimate(
            flops=8 * rows * keys * width,
            bytes_accessed=8 * rows * width,
            transcendentals=heads * rows * keys,
        ),
        name=name,
    )(*operands)


def output_kernel(ids, keep, got, w, *outs, half, kinds):
    step = pl.program_id(0)
    own_heads = keep.shape[1]
    mine = pl.multiple_of(ids[-1 + ids.shape[0]] * own_heads, own_heads)
    other = pl.multiple_of((1 - ids[-1 + ids.shape[0]]) * own_heads, own_heads)
    part = jnp.dot(keep[...], w[pl.ds(mine, own_heads), :], preferred_element_type=f32)
    part = part + jnp.dot(got[...], w[pl.ds(other, own_heads), :], preferred_element_type=f32)
    if kinds is None:
        outs[0][0] = part.astype(bf16)
        return
    for k, places in enumerate(kinds):

        @pl.when(step == k)
        def _(places=places):
            for group, (out, slot) in enumerate(places):
                piece = part[group * half : (group + 1) * half]
                outs[out][slot] = piece.astype(outs[out].dtype)


def output_projection(ids, core, keep, got, w_out, columns, pairwise, name):
    rows = keep.shape[0]
    count = w_out.shape[1] // columns
    scalars = jnp.concatenate([ids, core[None]]).astype(jnp.int32)
    full = lambda a: pl.BlockSpec(a.shape, lambda k, s: (0,) * a.ndim)
    half = rows // 2
    if pairwise:
        kinds = [
            [(1, 0), (3, 0)],
            [(0, 0), (3, 1)],
            [(1, 1), (2, 0)],
            [(0, 1), (2, 1)],
        ]
        out_shape = [
            jax.ShapeDtypeStruct((2, half, columns), dtype) for dtype in (bf16, f32, bf16, f32)
        ]
        out_specs = [pl.BlockSpec((2, half, columns), lambda k, s: (0, 0, 0))] * 4
    else:
        kinds = None
        out_shape = [jax.ShapeDtypeStruct((count, rows, columns), bf16)]
        out_specs = [pl.BlockSpec((1, rows, columns), lambda k, s: (k, 0, 0))]
    return pl.pallas_call(
        functools.partial(output_kernel, half=half, kinds=kinds),
        grid_spec=pltpu.PrefetchScalarGridSpec(
            num_scalar_prefetch=1,
            grid=(count,),
            in_specs=[
                full(keep), full(got),
                pl.BlockSpec((w_out.shape[0], columns), lambda k, s: (0, s[k])),
            ],
            out_specs=out_specs,
        ),
        out_shape=out_shape,
        compiler_params=pltpu.CompilerParams(vmem_limit_bytes=VMEM_LIMIT),
        cost_estimate=pl.CostEstimate(
            flops=2 * rows * w_out.size, bytes_accessed=2 * w_out.size, transcendentals=0
        ),
        name=name,
    )(scalars, keep, got, w_out)


def local(streams, doc_ids, mix_weight, mix_bias, attn_gain, w_qkv, w_out):
    n, n_streams, width = streams.shape
    tp = lax.axis_size("tp")
    seq = lax.axis_size("seq")
    model = width * tp
    shard = lax.axis_index("tp")
    seq_index = lax.axis_index("seq")
    core = seq_index % 2
    chip = seq_index // 2
    rows = 2 * n
    chunks = GATHER_CHUNKS
    m = n // chunks
    pairwise = tp == 4

    all_ids = gathered_ids(doc_ids)
    before = [jnp.sum((all_ids < d).astype(jnp.int32)) for d in range(DOCS)]

    def start_of(ids):
        start = jnp.full(ids.shape, before[0])
        for d in range(1, DOCS):
            start = jnp.where(ids >= d, before[d], start)
        return start

    def chunked(a):
        halves = jnp.where(core == 0, a, jnp.concatenate([a[n:], a[:n]]))
        return halves.reshape(2, chunks, m).transpose(1, 0, 2).reshape(rows)

    chip_ids = lax.dynamic_slice_in_dim(all_ids, chip * rows, rows)
    start = chunked(start_of(chip_ids))[:, None]
    place = jnp.arange(chunks, dtype=jnp.int32)[:, None, None] * m
    place = place + jnp.arange(m, dtype=jnp.int32)[None, None, :]
    side = (jnp.arange(2, dtype=jnp.int32)[None, :, None] + core) % 2
    in_chip = (place + side * n).reshape(rows)
    pos = (chip * rows + in_chip)[:, None]
    edges = jnp.arange(seq // 2, dtype=jnp.int32) * rows
    reach = jnp.max(edges - start_of(all_ids[::rows]))
    most = max(0, (seq * n // 2 - rows) // n)
    level = jnp.clip((reach - rows + n - 1) // n, 0, most)

    wide = streams.astype(f32)
    squares = jnp.sum(wide * wide, axis=(1, 2))
    logits = jnp.einsum("tsd,sdc->ct", wide, mix_weight, precision=lax.Precision.HIGHEST)
    summed = tp_sum(jnp.concatenate([logits, squares[None]], axis=0))
    root = jnp.sqrt(summed[-1] / (n_streams * model) + norm_eps)
    coef = summed[:-1] / root[None] + mix_bias[:, None]
    pre = jax.nn.sigmoid(coef[:n_streams])
    post = 2.0 * jax.nn.sigmoid(coef[n_streams : 2 * n_streams])
    raw = jnp.exp(coef[2 * n_streams :])
    mixing = doubly_stochastic(
        [[raw[i * n_streams + j] for j in range(n_streams)] for i in range(n_streams)]
    )
    pre_t = pre.T
    mixed = jnp.einsum("ts,tsd->td", pre_t, wide, precision=lax.Precision.HIGHEST).astype(bf16)

    w3 = jnp.transpose(w_qkv, (1, 0, 2))
    gain = attn_gain.reshape(tp, width)
    if pairwise:
        ids = jnp.stack([shard ^ k for k in range(tp)])
    else:
        ids = jnp.arange(tp)
    q_full = jnp.zeros((rows, (width // 2)), bf16)
    own_kv, near_kv = [], []
    for c in range(chunks):
        piece = mixed[c * m : (c + 1) * m]
        if pairwise:
            from_x = by_xor(piece, "tp", 1)
            from_y = by_xor(piece, "tp", 2)
            far_a = by_xor(from_y[: m // 2], "tp", 1)
            far_b = by_xor(from_x[m // 2 :], "tp", 2)
            own, rem = piece, jnp.concatenate([from_x, from_y, far_a, far_b], axis=0)
        else:
            every = lax.all_gather(piece, "tp", axis=0, tiled=True)
            own, rem = every[:m], every[m:]
        o_own, o_rem = by_xor(own, "seq", 1), by_xor(rem, "seq", 1)
        q_full, kv = project(ids, core, own, rem, o_own, o_rem, gain, w3, q_full, c)
        own_kv.append(kv)
        near_kv.append(next_chip(kv))

    key_pos = lambda base, c: base + in_chip[c * 2 * m : (c + 1) * 2 * m]
    own_pos = (chip * rows + in_chip)[None]
    state = attend(q_full, start, pos, own_pos, own_kv, None, m, False, "attend_own")
    near_base = (chip - 1) * rows
    early = chunks - 1
    near_pos = (near_base + in_chip)[None]
    state = attend(
        q_full, start, pos, near_pos[:, : early * 2 * m], near_kv[:early], state, m, False,
        "attend_near",
    )

    def finish(units, q_full, start, pos, state, near_kv):
        last_pos = near_pos[:, early * 2 * m :]
        if units == 0:
            return attend(q_full, start, pos, last_pos, near_kv[early:], state, m, True, "attend_last")
        parts = []
        for half in (1, 0):
            side = half ^ core
            parts.append(
                jnp.concatenate(
                    [lax.dynamic_slice_in_dim(kv, side * m, m, axis=1) for kv in near_kv], axis=1
                )
            )
        got, got_pos = [], []
        for u in range(units):
            parts[u % 2] = next_chip(parts[u % 2])
            got.append(parts[u % 2])
            base = (chip - 2 - u // 2) * rows + (1 - u % 2) * n
            got_pos.append((base + jnp.arange(n, dtype=jnp.int32))[None])
        state = attend(
            q_full, start, pos, last_pos, near_kv[early:], state, m, False, "attend_last"
        )
        for u in range(units):
            state = attend(
                q_full, start, pos, got_pos[u], [got[u]], state, m, u == units - 1,
                f"attend_far{u}",
            )
        return state

    if most == 0:
        keep, send = finish(0, q_full, start, pos, state, near_kv)
    else:
        keep, send = lax.switch(
            level,
            [functools.partial(finish, units) for units in range(most + 1)],
            q_full, start, pos, state, near_kv,
        )
    got = by_xor(send, "seq", 1)

    results = []
    r = n // SCATTER_CHUNKS
    sums = []
    for c in range(SCATTER_CHUNKS):
        cut = slice(c * r, (c + 1) * r)
        outs = output_projection(ids, core, keep[cut], got[cut], w_out, width, pairwise, f"output{c}")
        if pairwise:
            send_x, keep_x, send_y, keep_y = outs
            in_x = by_xor(send_x, "tp", 1).astype(f32)
            in_y = by_xor(send_y, "tp", 2).astype(f32)
            next_y = (keep_x[1] + in_x[1]).astype(bf16)
            next_x = (keep_y[1] + in_y[1]).astype(bf16)
            end_y = by_xor(next_y, "tp", 2).astype(f32)
            end_x = by_xor(next_x, "tp", 1).astype(f32)
            branch = jnp.concatenate(
                [keep_x[0] + in_x[0] + end_y, keep_y[0] + in_y[0] + end_x], axis=0
            )
        else:
            branch = lax.psum_scatter(outs[0], "tp", scatter_dimension=0, tiled=False).astype(f32)
        part = wide[cut]
        mix_t = jnp.transpose(mixing[:, :, cut], (2, 0, 1))
        carried = jnp.einsum("tij,tjd->tid", mix_t, part, precision=lax.Precision.HIGHEST)
        post_t = post[:, cut].T
        results.append((carried + post_t[:, :, None] * branch[:, None, :]).astype(bf16))
    return jnp.concatenate(results, axis=0)


def solution(mesh):
    in_specs = (
        P("seq", None, "tp"),
        P("seq"),
        P(None, "tp", None),
        P(),
        P(),
        P(None, None, "tp"),
        P("tp", None),
    )
    return jax.shard_map(
        local, mesh=mesh, in_specs=in_specs, out_specs=P("seq", None, "tp"), check_vma=False
    )
```

```python
import functools

import jax
import jax.numpy as jnp
from jax import lax
from jax.experimental import pallas as pl
from jax.experimental.pallas import tpu as pltpu
from jax.sharding import PartitionSpec as P

HEAD_DIM = 128
BALANCE_ROUNDS = 20
DOCS = 4
GATHER_CHUNKS = 2
SCATTER_CHUNKS = 2

masked_score = -1e30
norm_eps = 1e-06
VMEM_LIMIT = 60 * 1024 * 1024


bf16 = jnp.bfloat16
f32 = jnp.float32


def by_xor(value, axis, bit):
    count = lax.axis_size(axis)
    return lax.ppermute(value, axis, [(i, i ^ bit) for i in range(count)])


def next_chip(value):
    count = lax.axis_size("seq")
    return lax.ppermute(value, "seq", [(i, i + 2) for i in range(count - 2)])


def gathered_ids(doc_ids):
    count = lax.axis_size("seq")
    index = lax.axis_index("seq")
    held, bit, steps = doc_ids, 1, []
    while bit < count:
        other = by_xor(held, "seq", bit)
        mine_first = (index & bit) == 0
        held = jnp.concatenate(
            [jnp.where(mine_first, held, other), jnp.where(mine_first, other, held)]
        )
        bit *= 2
        steps.append(held)
    return steps


def tp_sum(value):
    count = lax.axis_size("tp")
    if count == 4:
        return (value + by_xor(value, "tp", 1)) + (by_xor(value, "tp", 2) + by_xor(value, "tp", 3))
    return lax.psum(value, "tp")


def doubly_stochastic(mixing):
    grid = jnp.stack([jnp.stack(row) for row in mixing])

    def balance_round(_, running):
        running = running / jnp.sum(running, axis=1, keepdims=True)
        return running / jnp.sum(running, axis=0, keepdims=True)

    return lax.fori_loop(0, BALANCE_ROUNDS, balance_round, grid)


def project_kernel(ids, *refs, counts, which, width):
    total = sum(sum(c) for c in counts)
    parts, (gain, w, out, gained, buf, sems) = list(refs[:total]), refs[total:]
    pieces = len(counts[0])
    copies = {}
    for k in range(pieces):
        for slot, third in enumerate(which):
            row = pl.multiple_of(ids[k] * width, width)
            copies[k, slot] = pltpu.make_async_copy(
                w.at[third, pl.ds(row, width), :],
                buf.at[slot, pl.ds(k * width, width), :],
                sems.at[slot * pieces + k],
            )
            copies[k, slot].start()
    starts = []
    for chunk in counts:
        starts.append(len(starts) and starts[-1] + sum(chunk_before))
        chunk_before = chunk
    height = gained.shape[0] // len(counts)
    squares = [None] * len(counts)
    accs = [None] * len(which)
    for k in range(pieces):
        span = slice(k * width, (k + 1) * width)
        g = gain[pl.ds(ids[k], 1), :]
        for i, chunk in enumerate(counts):
            row, sums = i * height, []
            begin = starts[i] + sum(chunk[:k])
            for part in parts[begin : begin + chunk[k]]:
                x = part[...].astype(f32)
                sums.append(jnp.sum(x * x, axis=1, keepdims=True))
                gained[row : row + part.shape[0], span] = (x * g).astype(bf16)
                row += part.shape[0]
            square = jnp.concatenate(sums, axis=0) if len(sums) > 1 else sums[0]
            squares[i] = square if k == 0 else squares[i] + square
        for slot in range(len(which)):
            copies[k, slot].wait()
            part = jnp.dot(gained[:, span], buf[slot, span], preferred_element_type=f32)
            accs[slot] = part if k == 0 else accs[slot] + part
    whole = jnp.concatenate(squares, axis=0) if len(squares) > 1 else squares[0]
    scale = lax.rsqrt(whole / (pieces * width) + norm_eps)
    for slot in range(len(which)):
        out[slot] = (accs[slot] * scale).astype(bf16)


def project(ids, chunks, gain, w3, which):
    pieces, width = gain.shape
    counts = [[len(piece) for piece in chunk] for chunk in chunks]
    parts = [part for chunk in chunks for piece in chunk for part in piece]
    m = sum(sum(part.shape[0] for part in chunk[0]) for chunk in chunks)
    full = lambda a: pl.BlockSpec(a.shape, lambda i, s: (0,) * a.ndim)
    return pl.pallas_call(
        functools.partial(project_kernel, counts=counts, which=which, width=width),
        grid_spec=pltpu.PrefetchScalarGridSpec(
            num_scalar_prefetch=1,
            grid=(1,),
            in_specs=[*map(full, parts), full(gain), pl.BlockSpec(memory_space=pl.ANY)],
            out_specs=pl.BlockSpec((len(which), m, width), lambda i, s: (0, 0, 0)),
            scratch_shapes=[
                pltpu.VMEM((m, pieces * width), bf16),
                pltpu.VMEM((len(which), pieces * width, width), bf16),
                pltpu.SemaphoreType.DMA((len(which) * pieces,)),
            ],
        ),
        out_shape=jax.ShapeDtypeStruct((len(which), m, width), bf16),
        compiler_params=pltpu.CompilerParams(vmem_limit_bytes=VMEM_LIMIT),
        cost_estimate=pl.CostEstimate(
            flops=2 * m * pieces * width * width * len(which),
            bytes_accessed=2 * pieces * width * width * len(which),
            transcendentals=0,
        ),
    )(ids, *parts, gain, w3)


def attend_kernel(q, marks, bases, *refs, spans, first, final, paired):
    kvs, refs = [], list(refs)
    for i in range(len(spans)):
        if paired:
            one, two = refs.pop(0), refs.pop(0)
            flag = bases[len(spans) + i] == 1
            kvs.append([jnp.where(flag, one[j], two[j]) for j in range(2)])
        else:
            kvs.append(refs.pop(0))
    if not first:
        ml_in, acc_in = refs[:2]
        refs = refs[2:]
    rows = q.shape[0]
    block = min(512, rows)
    factor = HEAD_DIM**-0.5

    @pl.loop(0, rows // block)
    def _(b):
        cut = pl.ds(pl.multiple_of(b * block, block), block)
        queries = q[cut, :]
        start, pos = marks[0:1, cut], marks[1:2, cut]
        scores = []
        for i, (kv, causal) in enumerate(zip(kvs, spans)):
            s = lax.dot_general(
                kv[0], queries, (((1,), (1,)), ((), ())), preferred_element_type=f32
            )
            where = lax.broadcasted_iota(jnp.int32, s.shape, 0)
            allowed = where >= start - bases[i]
            if causal:
                allowed = allowed & (where <= pos - bases[i])
            scores.append(jnp.where(allowed, s * factor, masked_score))
        top = functools.reduce(jnp.maximum, [jnp.max(s, axis=0, keepdims=True) for s in scores])
        if not first:
            old_top, old_sum = ml_in[0, 0:1, cut], ml_in[0, 1:2, cut]
            top = jnp.maximum(top, old_top)
        total, acc = None, None
        for s, kv in zip(scores, kvs):
            p = jnp.exp(s - top)
            row = jnp.sum(p, axis=0, keepdims=True)
            part = lax.dot_general(
                kv[1], p.astype(bf16),
                (((0,), (0,)), ((), ())), preferred_element_type=f32,
            )
            total = row if total is None else total + row
            acc = part if acc is None else acc + part
        if not first:
            rescale = jnp.exp(old_top - top)
            total = total + old_sum * rescale
            acc = acc + acc_in[0, :, cut] * rescale
        if final:
            refs[0][cut, :] = (acc / total).T.astype(bf16)
        else:
            ml_out, acc_out = refs
            ml_out[0, 0:1, cut] = top
            ml_out[0, 1:2, cut] = total
            acc_out[0, :, cut] = acc


def attend(q, marks, kvs, bases, spans, state, final):
    rows, width = q.shape
    heads = width // HEAD_DIM
    first = state is None
    paired = isinstance(kvs[0], tuple)
    if paired:
        kvs = [kv for pair in kvs for kv in pair]
    keys = sum(kv.shape[1] for kv in kvs)
    in_specs = [
        pl.BlockSpec((rows, HEAD_DIM), lambda h: (0, h)),
        pl.BlockSpec(marks.shape, lambda h: (0, 0)),
        pl.BlockSpec(memory_space=pltpu.SMEM),
    ]
    in_specs += [pl.BlockSpec((2, kv.shape[1], HEAD_DIM), lambda h: (0, 0, h)) for kv in kvs]
    operands = [q, marks, bases, *kvs]
    state_shapes = [(heads, 8, rows), (heads, HEAD_DIM, rows)]
    state_specs = [pl.BlockSpec((1,) + s[1:], lambda h: (h, 0, 0)) for s in state_shapes]
    aliases = {}
    if not first:
        if not final:
            aliases = {len(operands): 0, len(operands) + 1: 1}
        operands += list(state)
        in_specs += state_specs
    if final:
        out_specs = pl.BlockSpec((rows, HEAD_DIM), lambda h: (0, h))
        out_shape = jax.ShapeDtypeStruct((rows, width), bf16)
    else:
        out_specs = state_specs
        out_shape = [jax.ShapeDtypeStruct(s, f32) for s in state_shapes]
    return pl.pallas_call(
        functools.partial(attend_kernel, spans=spans, first=first, final=final, paired=paired),
        grid=(heads,),
        in_specs=in_specs,
        out_specs=out_specs,
        out_shape=out_shape,
        input_output_aliases=aliases,
        compiler_params=pltpu.CompilerParams(vmem_limit_bytes=VMEM_LIMIT),
        cost_estimate=pl.CostEstimate(
            flops=8 * rows * keys * width,
            bytes_accessed=8 * rows * width,
            transcendentals=heads * rows * keys,
        ),
    )(*operands)


def output_kernel(ids, context, w, *refs, half, kinds, count, columns):
    outs, (buf, sems) = refs[:-2], refs[-2:]
    copies = []
    for k in range(count):
        col = pl.multiple_of(ids[k] * columns, columns)
        copy = pltpu.make_async_copy(w.at[:, pl.ds(col, columns)], buf.at[k], sems.at[k])
        copy.start()
        copies.append(copy)
    for k in range(count):
        copies[k].wait()
        part = jnp.dot(context[...], buf[k], preferred_element_type=f32)
        if kinds is None:
            outs[0][k] = part.astype(bf16)
            continue
        for group, (out, slot) in enumerate(kinds[k]):
            piece = part[group * half : (group + 1) * half]
            outs[out][slot] = piece.astype(outs[out].dtype)


def output_projection(ids, context, chunk, rows, w_out, columns, pairwise):
    count = w_out.shape[1] // columns
    half = rows // 2
    kinds = None
    if pairwise:
        kinds = [
            [(1, 0), (3, 0)],
            [(0, 0), (3, 1)],
            [(1, 1), (2, 0)],
            [(0, 1), (2, 1)],
        ]
        out_shape = [
            jax.ShapeDtypeStruct((2, half, columns), dtype) for dtype in (bf16, f32, bf16, f32)
        ]
    else:
        out_shape = [jax.ShapeDtypeStruct((count, rows, columns), bf16)]
    out_specs = [pl.BlockSpec(s.shape, lambda i, s: (0, 0, 0)) for s in out_shape]
    return pl.pallas_call(
        functools.partial(output_kernel, half=half, kinds=kinds, count=count, columns=columns),
        grid_spec=pltpu.PrefetchScalarGridSpec(
            num_scalar_prefetch=1,
            grid=(1,),
            in_specs=[
                pl.BlockSpec((rows, context.shape[1]), lambda i, s: (chunk, 0)),
                pl.BlockSpec(memory_space=pl.ANY),
            ],
            out_specs=out_specs,
            scratch_shapes=[
                pltpu.VMEM((count, w_out.shape[0], columns), bf16),
                pltpu.SemaphoreType.DMA((count,)),
            ],
        ),
        out_shape=out_shape,
        compiler_params=pltpu.CompilerParams(vmem_limit_bytes=VMEM_LIMIT),
        cost_estimate=pl.CostEstimate(
            flops=2 * rows * w_out.size, bytes_accessed=2 * w_out.size, transcendentals=0
        ),
    )(ids, context, w_out)


def tie(value, *after):
    return lax.optimization_barrier((value, *after))[0]


def local(streams, doc_ids, mix_weight, mix_bias, attn_gain, w_qkv, w_out):
    n, n_streams, width = streams.shape
    tp = lax.axis_size("tp")
    seq = lax.axis_size("seq")
    model = width * tp
    shard = lax.axis_index("tp")
    seq_index = lax.axis_index("seq")
    core = seq_index % 2
    chip = seq_index // 2
    rows = 2 * n
    chunks = GATHER_CHUNKS
    m = n // chunks
    pairwise = tp == 4

    id_steps = gathered_ids(doc_ids)
    all_ids = id_steps[-1]
    before = [jnp.sum((all_ids < d).astype(jnp.int32)) for d in range(DOCS)]

    def start_of(ids):
        start = jnp.full(ids.shape, before[0])
        for d in range(1, DOCS):
            start = jnp.where(ids >= d, before[d], start)
        return start

    marks = jnp.concatenate(
        [
            start_of(doc_ids)[None],
            (seq_index * n + jnp.arange(n, dtype=jnp.int32))[None],
            jnp.zeros((6, n), jnp.int32),
        ]
    )
    edges = jnp.arange(seq // 2, dtype=jnp.int32) * rows
    reach = jnp.max(edges - start_of(all_ids[::rows]))
    most = max(0, (seq * n // 2 - rows) // m)
    level = jnp.clip((reach - rows + m - 1) // m, 0, most)

    wide = streams.astype(f32)
    squares = jnp.sum(wide * wide, axis=(1, 2))
    next_wide = tie(streams, id_steps[0], squares).astype(f32)
    logits = jnp.einsum("tsd,sdc->ct", next_wide, mix_weight, precision=lax.Precision.HIGHEST)
    logits = tie(logits, all_ids)
    summed = tp_sum(jnp.concatenate([logits, squares[None]], axis=0))
    root = jnp.sqrt(summed[-1] / (n_streams * model) + norm_eps)
    coef = summed[:-1] / root[None] + mix_bias[:, None]
    pre = jax.nn.sigmoid(coef[:n_streams])
    post = 2.0 * jax.nn.sigmoid(coef[n_streams : 2 * n_streams])
    raw = jnp.exp(coef[2 * n_streams :])
    pre_t = pre.T

    w3 = jnp.transpose(w_qkv, (1, 0, 2))
    gain = attn_gain.reshape(tp, width)
    if pairwise:
        ids = jnp.stack([shard ^ k for k in range(tp)])
    else:
        ids = jnp.arange(tp)
    mixed = [
        jnp.einsum(
            "ts,tsd->td", pre_t[c * m : (c + 1) * m], wide[c * m : (c + 1) * m],
            precision=lax.Precision.HIGHEST,
        ).astype(bf16)
        for c in range(chunks)
    ]
    raw = tie(raw, mixed[-1])
    mixing = doubly_stochastic(
        [[raw[i * n_streams + j] for j in range(n_streams)] for i in range(n_streams)]
    )
    pieces = []
    for c in range(chunks):
        if pairwise:
            from_x = by_xor(mixed[c], "tp", 1)
            from_y = by_xor(mixed[c], "tp", 2)
            pieces.append([[mixed[c]], [from_x], [from_y]])
        else:
            every = lax.all_gather(mixed[c], "tp", axis=0)
            pieces.append([[every[k]] for k in range(tp)])
    own_kv, other_kv, near_own, near_other = [], [], [], []
    for c in range(chunks):
        if pairwise:
            from_x, from_y = pieces[c][1][0], pieces[c][2][0]
            after = mixed[1:] if c == 0 else [own_kv[c - 1]]
            from_x, from_y = lax.optimization_barrier((from_x, from_y, *after))[:2]
            pieces[c].append([by_xor(from_y[: m // 2], "tp", 1), by_xor(from_x[m // 2 :], "tp", 2)])
        kv = project(ids, [pieces[c]], gain, w3, (1, 2))
        own_kv.append(kv)
        near_own.append(next_chip(kv))
        other_kv.append(by_xor(kv, "seq", 1))
    q = project(ids, pieces, gain, w3, (0,))[0]
    early = chunks // 2
    for c in range(early):
        near_other.append(by_xor(tie(near_own[c], q), "seq", 1))

    def base_of(where, which, c):
        return where * rows + which * n + c * m

    def table(bases):
        return jnp.stack([jnp.asarray(b, jnp.int32) for b in bases])

    bases = [base_of(chip, which, c) for which in (core, 1 - core) for c in range(chunks)]
    bases += [base_of(chip - 1, which, c) for which in (core, 1 - core) for c in range(early)]
    state = attend(
        q, marks, own_kv + other_kv + near_own[:early] + near_other[:early], table(bases),
        [True] * (2 * chunks) + [False] * (2 * early), None, False,
    )
    for c in range(early, chunks):
        near_other.append(by_xor(tie(near_own[c], *state), "seq", 1))

    def finish(units, q, marks, state, near_own, near_other):
        late = near_own[early:] + near_other[early:]
        bases = [
            base_of(chip - 1, which, c) for which in (core, 1 - core) for c in range(early, chunks)
        ]
        if units == 0:
            return attend(q, marks, late, table(bases), [False] * len(late), state, True)
        held = {(which, c): near_own[c] for which in (0, 1) for c in range(chunks)}
        far, far_bases = [], []
        for u in range(units):
            hop, rest = 2 + u // (2 * chunks), u % (2 * chunks)
            which, c = 1 - rest // chunks, chunks - 1 - rest % chunks
            sent = lax.ppermute(
                held[which, c], "seq", [(i, i + 2) for i in range(which, seq - 2, 2)]
            )
            held[which, c] = sent
            far.append((which, sent))
            far_bases.append(base_of(chip - hop, which, c))
        state = attend(q, marks, late, table(bases), [False] * len(late), state, False)
        pairs = []
        for which, sent in far:
            shown = lax.ppermute(
                tie(sent, *state), "seq", [(i, i ^ 1) for i in range(which, seq, 2)]
            )
            pairs.append((sent, shown))
        far_bases += [(core == which).astype(jnp.int32) for which, _ in far]
        return attend(q, marks, pairs, table(far_bases), [False] * units, state, True)

    if most == 0:
        context = finish(0, q, marks, state, near_own, near_other)
    else:
        context = lax.switch(
            level,
            [functools.partial(finish, units) for units in range(most + 1)],
            q, marks, state, near_own, near_other,
        )

    r = n // SCATTER_CHUNKS
    firsts = []
    for c in range(SCATTER_CHUNKS):
        outs = output_projection(ids, context, c, r, w_out, width, pairwise)
        if pairwise:
            send_x, keep_x, send_y, keep_y = outs
            firsts.append(
                (
                    keep_x, by_xor(send_x, "tp", 1),
                    keep_y, by_xor(send_y, "tp", 2),
                )
            )
        else:
            firsts.append(lax.psum_scatter(outs[0], "tp", scatter_dimension=0, tiled=False))
    seconds = []
    for c in range(SCATTER_CHUNKS):
        if pairwise:
            keep_x, in_x, keep_y, in_y = firsts[c]
            next_y = (keep_x[1] + in_x[1].astype(f32)).astype(bf16)
            next_x = (keep_y[1] + in_y[1].astype(f32)).astype(bf16)
            seconds.append((by_xor(next_y, "tp", 2), by_xor(next_x, "tp", 1)))
    pieces = []
    for c in range(SCATTER_CHUNKS):
        if pairwise:
            keep_x, in_x, keep_y, in_y = firsts[c]
            end_y, end_x = seconds[c]
            pieces.append(keep_x[0] + in_x[0].astype(f32) + end_y.astype(f32))
            pieces.append(keep_y[0] + in_y[0].astype(f32) + end_x.astype(f32))
        else:
            pieces.append(firsts[c].astype(f32))
    branch = jnp.concatenate(pieces, axis=0)
    mix_t = jnp.transpose(mixing, (2, 0, 1))
    carried = jnp.einsum("tij,tjd->tid", mix_t, wide, precision=lax.Precision.HIGHEST)
    return (carried + post.T[:, :, None] * branch[:, None, :]).astype(bf16)


def solution(mesh):
    in_specs = (
        P("seq", None, "tp"),
        P("seq"),
        P(None, "tp", None),
        P(),
        P(),
        P(None, None, "tp"),
        P("tp", None),
    )

    return jax.shard_map(
        local, mesh=mesh, in_specs=in_specs, out_specs=P("seq", None, "tp"), check_vma=False
    )
```

```python
import functools
import math

import jax
import jax.numpy as jnp
from jax import lax
from jax.experimental import pallas as pl
from jax.experimental.pallas import tpu as pltpu
from jax.sharding import PartitionSpec as P

HEAD_DIM = 128
BALANCE_ROUNDS = 20
DOCS = 4
GATHER_CHUNKS = 2
SCATTER_CHUNKS = 2

masked_score = -1e30
norm_eps = 1e-06
VMEM_LIMIT = 60 * 1024 * 1024


bf16 = jnp.bfloat16
f32 = jnp.float32


def by_xor(value, axis, bit):
    count = lax.axis_size(axis)
    return lax.ppermute(value, axis, [(i, i ^ bit) for i in range(count)])


def next_chip(value):
    count = lax.axis_size("seq")
    return lax.ppermute(value, "seq", [(i, i + 2) for i in range(count - 2)])


def gathered_ids(doc_ids):
    count = lax.axis_size("seq")
    index = lax.axis_index("seq")
    held, bit, steps = doc_ids, 1, []
    while bit < count:
        other = by_xor(held, "seq", bit)
        mine_first = (index & bit) == 0
        held = jnp.concatenate(
            [jnp.where(mine_first, held, other), jnp.where(mine_first, other, held)]
        )
        bit *= 2
        steps.append(held)
    return steps


def tp_sum(value):
    count = lax.axis_size("tp")
    if count == 4:
        return (value + by_xor(value, "tp", 1)) + (by_xor(value, "tp", 2) + by_xor(value, "tp", 3))
    return lax.psum(value, "tp")


def doubly_stochastic(mixing):
    grid = jnp.stack([jnp.stack(row) for row in mixing])

    def balance_round(_, running):
        running = running / jnp.sum(running, axis=1, keepdims=True)
        return running / jnp.sum(running, axis=0, keepdims=True)

    return lax.fori_loop(0, BALANCE_ROUNDS, balance_round, grid)


def project_kernel(ids, *refs, counts, which, width):
    total = sum(sum(c) for c in counts)
    parts, (gain, w, out, gained, buf, sems) = list(refs[:total]), refs[total:]
    pieces = len(counts[0])
    copies = {}
    for k in range(pieces):
        for slot, third in enumerate(which):
            row = pl.multiple_of(ids[k] * width, width)
            copies[k, slot] = pltpu.make_async_copy(
                w.at[third, pl.ds(row, width), :],
                buf.at[slot, pl.ds(k * width, width), :],
                sems.at[slot * pieces + k],
            )
            copies[k, slot].start()
    starts = []
    for chunk in counts:
        starts.append(len(starts) and starts[-1] + sum(chunk_before))
        chunk_before = chunk
    height = gained.shape[0] // len(counts)
    squares = [None] * len(counts)
    accs = [None] * len(which)
    for k in range(pieces):
        span = slice(k * width, (k + 1) * width)
        g = gain[pl.ds(ids[k], 1), :]
        for i, chunk in enumerate(counts):
            row, sums = i * height, []
            begin = starts[i] + sum(chunk[:k])
            for part in parts[begin : begin + chunk[k]]:
                x = part[...].astype(f32)
                sums.append(jnp.sum(x * x, axis=1, keepdims=True))
                gained[row : row + part.shape[0], span] = (x * g).astype(bf16)
                row += part.shape[0]
            square = jnp.concatenate(sums, axis=0) if len(sums) > 1 else sums[0]
            squares[i] = square if k == 0 else squares[i] + square
        for slot in range(len(which)):
            copies[k, slot].wait()
            part = jnp.dot(gained[:, span], buf[slot, span], preferred_element_type=f32)
            accs[slot] = part if k == 0 else accs[slot] + part
    whole = jnp.concatenate(squares, axis=0) if len(squares) > 1 else squares[0]
    scale = lax.rsqrt(whole / (pieces * width) + norm_eps)
    for slot in range(len(which)):
        out[slot] = (accs[slot] * scale).astype(bf16)


def project(ids, chunks, gain, w3, which):
    pieces, width = gain.shape
    counts = [[len(piece) for piece in chunk] for chunk in chunks]
    parts = [part for chunk in chunks for piece in chunk for part in piece]
    m = sum(sum(part.shape[0] for part in chunk[0]) for chunk in chunks)
    full = lambda a: pl.BlockSpec(a.shape, lambda i, s: (0,) * a.ndim)
    return pl.pallas_call(
        functools.partial(project_kernel, counts=counts, which=which, width=width),
        grid_spec=pltpu.PrefetchScalarGridSpec(
            num_scalar_prefetch=1,
            grid=(1,),
            in_specs=[*map(full, parts), full(gain), pl.BlockSpec(memory_space=pl.ANY)],
            out_specs=pl.BlockSpec((len(which), m, width), lambda i, s: (0, 0, 0)),
            scratch_shapes=[
                pltpu.VMEM((m, pieces * width), bf16),
                pltpu.VMEM((len(which), pieces * width, width), bf16),
                pltpu.SemaphoreType.DMA((len(which) * pieces,)),
            ],
        ),
        out_shape=jax.ShapeDtypeStruct((len(which), m, width), bf16),
        compiler_params=pltpu.CompilerParams(vmem_limit_bytes=VMEM_LIMIT),
        cost_estimate=pl.CostEstimate(
            flops=2 * m * pieces * width * width * len(which),
            bytes_accessed=2 * pieces * width * width * len(which),
            transcendentals=0,
        ),
    )(ids, *parts, gain, w3)


def attend_kernel(q, marks, bases, *refs, spans, first, final, paired):
    kvs, refs = [], list(refs)
    for i in range(len(spans)):
        if paired:
            one, two = refs.pop(0), refs.pop(0)
            flag = bases[len(spans) + i] == 1
            kvs.append([jnp.where(flag, one[j], two[j]) for j in range(2)])
        else:
            kvs.append(refs.pop(0))
    if not first:
        ml_in, acc_in = refs[:2]
        refs = refs[2:]
    rows = q.shape[0]
    block = min(512, rows)
    factor = HEAD_DIM**-0.5 * math.log2(math.e)

    @pl.loop(0, rows // block)
    def _(b):
        cut = pl.ds(pl.multiple_of(b * block, block), block)
        queries = q[cut, :]
        start, pos = marks[0:1, cut], marks[1:2, cut]
        scores = []
        for i, (kv, causal) in enumerate(zip(kvs, spans)):
            s = lax.dot_general(
                kv[0], queries, (((1,), (1,)), ((), ())), preferred_element_type=f32
            )
            where = lax.broadcasted_iota(jnp.int32, s.shape, 0)
            allowed = where >= start - bases[i]
            if causal:
                allowed = allowed & (where <= pos - bases[i])
            scores.append(jnp.where(allowed, s, masked_score))
        top = functools.reduce(jnp.maximum, [jnp.max(s, axis=0, keepdims=True) for s in scores])
        if not first:
            old_top, old_sum = ml_in[0, 0:1, cut], ml_in[0, 1:2, cut]
            top = jnp.maximum(top, old_top)
        total, acc = None, None
        for s, kv in zip(scores, kvs):
            p = jnp.exp2((s - top) * factor)
            row = jnp.sum(p, axis=0, keepdims=True)
            part = lax.dot_general(
                kv[1], p.astype(bf16),
                (((0,), (0,)), ((), ())), preferred_element_type=f32,
            )
            total = row if total is None else total + row
            acc = part if acc is None else acc + part
        if not first:
            rescale = jnp.exp2((old_top - top) * factor)
            total = total + old_sum * rescale
            acc = acc + acc_in[0, :, cut] * rescale
        if final:
            refs[0][cut, :] = (acc / total).T.astype(bf16)
        else:
            ml_out, acc_out = refs
            ml_out[0, 0:1, cut] = top
            ml_out[0, 1:2, cut] = total
            acc_out[0, :, cut] = acc


def attend(q, marks, kvs, bases, spans, state, final):
    rows, width = q.shape
    heads = width // HEAD_DIM
    first = state is None
    paired = isinstance(kvs[0], tuple)
    if paired:
        kvs = [kv for pair in kvs for kv in pair]
    keys = sum(kv.shape[1] for kv in kvs)
    in_specs = [
        pl.BlockSpec((rows, HEAD_DIM), lambda h: (0, h)),
        pl.BlockSpec(marks.shape, lambda h: (0, 0)),
        pl.BlockSpec(memory_space=pltpu.SMEM),
    ]
    in_specs += [pl.BlockSpec((2, kv.shape[1], HEAD_DIM), lambda h: (0, 0, h)) for kv in kvs]
    operands = [q, marks, bases, *kvs]
    state_shapes = [(heads, 8, rows), (heads, HEAD_DIM, rows)]
    state_specs = [pl.BlockSpec((1,) + s[1:], lambda h: (h, 0, 0)) for s in state_shapes]
    aliases = {}
    if not first:
        if not final:
            aliases = {len(operands): 0, len(operands) + 1: 1}
        operands += list(state)
        in_specs += state_specs
    if final:
        out_specs = pl.BlockSpec((rows, HEAD_DIM), lambda h: (0, h))
        out_shape = jax.ShapeDtypeStruct((rows, width), bf16)
    else:
        out_specs = state_specs
        out_shape = [jax.ShapeDtypeStruct(s, f32) for s in state_shapes]
    return pl.pallas_call(
        functools.partial(attend_kernel, spans=spans, first=first, final=final, paired=paired),
        grid=(heads,),
        in_specs=in_specs,
        out_specs=out_specs,
        out_shape=out_shape,
        input_output_aliases=aliases,
        compiler_params=pltpu.CompilerParams(vmem_limit_bytes=VMEM_LIMIT),
        cost_estimate=pl.CostEstimate(
            flops=8 * rows * keys * width,
            bytes_accessed=8 * rows * width,
            transcendentals=heads * rows * keys,
        ),
    )(*operands)


def output_kernel(ids, context, w, *refs, half, kinds, count, columns):
    outs, (buf, sems) = refs[:-2], refs[-2:]
    copies = []
    for k in range(count):
        col = pl.multiple_of(ids[k] * columns, columns)
        copy = pltpu.make_async_copy(w.at[:, pl.ds(col, columns)], buf.at[k], sems.at[k])
        copy.start()
        copies.append(copy)
    for k in range(count):
        copies[k].wait()
        part = jnp.dot(context[...], buf[k], preferred_element_type=f32)
        if kinds is None:
            outs[0][k] = part.astype(bf16)
            continue
        for group, (out, slot) in enumerate(kinds[k]):
            piece = part[group * half : (group + 1) * half]
            outs[out][slot] = piece.astype(outs[out].dtype)


def output_projection(ids, context, chunk, rows, w_out, columns, pairwise):
    count = w_out.shape[1] // columns
    half = rows // 2
    kinds = None
    if pairwise:
        kinds = [
            [(1, 0), (3, 0)],
            [(0, 0), (3, 1)],
            [(1, 1), (2, 0)],
            [(0, 1), (2, 1)],
        ]
        out_shape = [
            jax.ShapeDtypeStruct((2, half, columns), dtype) for dtype in (bf16, f32, bf16, f32)
        ]
    else:
        out_shape = [jax.ShapeDtypeStruct((count, rows, columns), bf16)]
    out_specs = [pl.BlockSpec(s.shape, lambda i, s: (0, 0, 0)) for s in out_shape]
    return pl.pallas_call(
        functools.partial(output_kernel, half=half, kinds=kinds, count=count, columns=columns),
        grid_spec=pltpu.PrefetchScalarGridSpec(
            num_scalar_prefetch=1,
            grid=(1,),
            in_specs=[
                pl.BlockSpec((rows, context.shape[1]), lambda i, s: (chunk, 0)),
                pl.BlockSpec(memory_space=pl.ANY),
            ],
            out_specs=out_specs,
            scratch_shapes=[
                pltpu.VMEM((count, w_out.shape[0], columns), bf16),
                pltpu.SemaphoreType.DMA((count,)),
            ],
        ),
        out_shape=out_shape,
        compiler_params=pltpu.CompilerParams(vmem_limit_bytes=VMEM_LIMIT),
        cost_estimate=pl.CostEstimate(
            flops=2 * rows * w_out.size, bytes_accessed=2 * w_out.size, transcendentals=0
        ),
    )(ids, context, w_out)


def tie(value, *after):
    return lax.optimization_barrier((value, *after))[0]


def local(streams, doc_ids, mix_weight, mix_bias, attn_gain, w_qkv, w_out):
    n, n_streams, width = streams.shape
    tp = lax.axis_size("tp")
    seq = lax.axis_size("seq")
    model = width * tp
    shard = lax.axis_index("tp")
    seq_index = lax.axis_index("seq")
    core = seq_index % 2
    chip = seq_index // 2
    rows = 2 * n
    chunks = GATHER_CHUNKS
    m = n // chunks
    pairwise = tp == 4

    id_steps = gathered_ids(doc_ids)
    all_ids = id_steps[-1]
    before = [jnp.sum((all_ids < d).astype(jnp.int32)) for d in range(DOCS)]

    def start_of(ids):
        start = jnp.full(ids.shape, before[0])
        for d in range(1, DOCS):
            start = jnp.where(ids >= d, before[d], start)
        return start

    marks = jnp.concatenate(
        [
            start_of(doc_ids)[None],
            (seq_index * n + jnp.arange(n, dtype=jnp.int32))[None],
            jnp.zeros((6, n), jnp.int32),
        ]
    )
    edges = jnp.arange(seq // 2, dtype=jnp.int32) * rows
    reach = jnp.max(edges - start_of(all_ids[::rows]))
    most = max(0, (seq * n // 2 - rows) // m)
    level = jnp.clip((reach - rows + m - 1) // m, 0, most)

    wide = streams.astype(f32)
    squares = jnp.sum(wide * wide, axis=(1, 2))
    next_wide = tie(streams, squares).astype(f32)
    logits = jnp.einsum("tsd,sdc->ct", next_wide, mix_weight, precision=lax.Precision.HIGHEST)
    summed = tp_sum(jnp.concatenate([logits, squares[None]], axis=0))
    root = jnp.sqrt(summed[-1] / (n_streams * model) + norm_eps)
    coef = summed[:-1] / root[None] + mix_bias[:, None]
    pre = jax.nn.sigmoid(coef[:n_streams])
    post = 2.0 * jax.nn.sigmoid(coef[n_streams : 2 * n_streams])
    raw = jnp.exp(coef[2 * n_streams :])
    pre_t = pre.T

    w3 = jnp.transpose(w_qkv, (1, 0, 2))
    gain = attn_gain.reshape(tp, width)
    if pairwise:
        ids = jnp.stack([shard ^ k for k in range(tp)])
    else:
        ids = jnp.arange(tp)
    mixed = [
        jnp.einsum(
            "ts,tsd->td", pre_t[c * m : (c + 1) * m], wide[c * m : (c + 1) * m],
            precision=lax.Precision.HIGHEST,
        ).astype(bf16)
        for c in range(chunks)
    ]
    raw = tie(raw, mixed[-1])
    mixing = doubly_stochastic(
        [[raw[i * n_streams + j] for j in range(n_streams)] for i in range(n_streams)]
    )
    pieces = []
    for c in range(chunks):
        if pairwise:
            from_x = by_xor(mixed[c], "tp", 1)
            from_y = by_xor(mixed[c], "tp", 2)
            pieces.append([[mixed[c]], [from_x], [from_y]])
        else:
            every = lax.all_gather(mixed[c], "tp", axis=0)
            pieces.append([[every[k]] for k in range(tp)])
    own_kv, other_kv, near_own, near_other = [], [], [], []
    for c in range(chunks):
        if pairwise:
            from_x, from_y = pieces[c][1][0], pieces[c][2][0]
            after = [*mixed[1:], id_steps[1]] if c == 0 else [own_kv[c - 1], marks, level]
            from_x, from_y = lax.optimization_barrier((from_x, from_y, *after))[:2]
            pieces[c].append([by_xor(from_y[: m // 2], "tp", 1), by_xor(from_x[m // 2 :], "tp", 2)])
        if c == 0:
            pieces[0][0][0] = tie(pieces[0][0][0], all_ids)
        kv = project(ids, [pieces[c]], gain, w3, (1, 2))
        own_kv.append(kv)
        near_own.append(next_chip(kv))
        other_kv.append(by_xor(kv, "seq", 1))
    q = project(ids, pieces, gain, w3, (0,))[0]
    early = chunks // 2
    for c in range(early):
        near_other.append(by_xor(tie(near_own[c], q), "seq", 1))

    def base_of(where, which, c):
        return where * rows + which * n + c * m

    def table(bases):
        return jnp.stack([jnp.asarray(b, jnp.int32) for b in bases])

    bases = [base_of(chip, core, c) for c in range(chunks)]
    bases += [jnp.where(core == 1, base_of(chip, 0, c), -(1 << 29)) for c in range(chunks)]
    bases += [base_of(chip - 1, which, c) for which in (core, 1 - core) for c in range(early)]
    state = attend(
        q, marks, own_kv + other_kv + near_own[:early] + near_other[:early], table(bases),
        [True] * chunks + [False] * (chunks + 2 * early), None, False,
    )
    for c in range(early, chunks):
        near_other.append(by_xor(tie(near_own[c], *state), "seq", 1))

    def finish(units, q, marks, state, near_own, near_other):
        late = near_own[early:] + near_other[early:]
        bases = [
            base_of(chip - 1, which, c) for which in (core, 1 - core) for c in range(early, chunks)
        ]
        if units == 0:
            return attend(q, marks, late, table(bases), [False] * len(late), state, True)
        held = {(which, c): near_own[c] for which in (0, 1) for c in range(chunks)}
        far, far_bases = [], []
        for u in range(units):
            hop, rest = 2 + u // (2 * chunks), u % (2 * chunks)
            which, c = 1 - rest // chunks, chunks - 1 - rest % chunks
            sent = lax.ppermute(
                held[which, c], "seq", [(i, i + 2) for i in range(which, seq - 2, 2)]
            )
            held[which, c] = sent
            far.append((which, sent))
            far_bases.append(base_of(chip - hop, which, c))
        state = attend(q, marks, late, table(bases), [False] * len(late), state, False)
        pairs = []
        for which, sent in far:
            shown = lax.ppermute(
                tie(sent, *state), "seq", [(i, i ^ 1) for i in range(which, seq, 2)]
            )
            pairs.append((sent, shown))
        far_bases += [(core == which).astype(jnp.int32) for which, _ in far]
        return attend(q, marks, pairs, table(far_bases), [False] * units, state, True)

    if most == 0:
        context = finish(0, q, marks, state, near_own, near_other)
    else:
        context = lax.switch(
            level,
            [functools.partial(finish, units) for units in range(most + 1)],
            q, marks, state, near_own, near_other,
        )

    r = n // SCATTER_CHUNKS
    firsts = []
    for c in range(SCATTER_CHUNKS):
        outs = output_projection(ids, context, c, r, w_out, width, pairwise)
        if pairwise:
            send_x, keep_x, send_y, keep_y = outs
            firsts.append(
                (
                    keep_x, by_xor(send_x, "tp", 1),
                    keep_y, by_xor(send_y, "tp", 2),
                )
            )
        else:
            firsts.append(lax.psum_scatter(outs[0], "tp", scatter_dimension=0, tiled=False))
    seconds = []
    for c in range(SCATTER_CHUNKS):
        if pairwise:
            keep_x, in_x, keep_y, in_y = firsts[c]
            next_y = (keep_x[1] + in_x[1].astype(f32)).astype(bf16)
            next_x = (keep_y[1] + in_y[1].astype(f32)).astype(bf16)
            seconds.append((by_xor(next_y, "tp", 2), by_xor(next_x, "tp", 1)))
    pieces = []
    for c in range(SCATTER_CHUNKS):
        if pairwise:
            keep_x, in_x, keep_y, in_y = firsts[c]
            end_y, end_x = seconds[c]
            pieces.append(keep_x[0] + in_x[0].astype(f32) + end_y.astype(f32))
            pieces.append(keep_y[0] + in_y[0].astype(f32) + end_x.astype(f32))
        else:
            pieces.append(firsts[c].astype(f32))
    branch = jnp.concatenate(pieces, axis=0)
    mix_t = jnp.transpose(mixing, (2, 0, 1))
    carried = jnp.einsum("tij,tjd->tid", mix_t, wide, precision=lax.Precision.HIGHEST)
    return (carried + post.T[:, :, None] * branch[:, None, :]).astype(bf16)


def solution(mesh):
    in_specs = (
        P("seq", None, "tp"),
        P("seq"),
        P(None, "tp", None),
        P(),
        P(),
        P(None, None, "tp"),
        P("tp", None),
    )

    return jax.shard_map(
        local, mesh=mesh, in_specs=in_specs, out_specs=P("seq", None, "tp"), check_vma=False
    )
```

```python
import functools
import math

import jax
import jax.numpy as jnp
from jax import lax
from jax.experimental import pallas as pl
from jax.experimental.pallas import tpu as pltpu
from jax.sharding import PartitionSpec as P

HEAD_DIM = 128
BALANCE_ROUNDS = 20
DOCS = 4
GATHER_CHUNKS = 2
SCATTER_CHUNKS = 2

masked_score = -1e30
norm_eps = 1e-06
VMEM_LIMIT = 60 * 1024 * 1024


bf16 = jnp.bfloat16
f32 = jnp.float32


def by_xor(value, axis, bit):
    count = lax.axis_size(axis)
    return lax.ppermute(value, axis, [(i, i ^ bit) for i in range(count)])


def next_chip(value):
    count = lax.axis_size("seq")
    return lax.ppermute(value, "seq", [(i, i + 2) for i in range(count - 2)])


def gathered_ids(doc_ids):
    count = lax.axis_size("seq")
    index = lax.axis_index("seq")
    held, bit, steps = doc_ids, 1, []
    while bit < count:
        other = by_xor(held, "seq", bit)
        mine_first = (index & bit) == 0
        held = jnp.concatenate(
            [jnp.where(mine_first, held, other), jnp.where(mine_first, other, held)]
        )
        bit *= 2
        steps.append(held)
    return steps


def tp_sum(value):
    count = lax.axis_size("tp")
    if count == 4:
        return (value + by_xor(value, "tp", 1)) + (by_xor(value, "tp", 2) + by_xor(value, "tp", 3))
    return lax.psum(value, "tp")


def doubly_stochastic(mixing):
    grid = jnp.stack([jnp.stack(row) for row in mixing])

    def balance_round(_, running):
        running = running / jnp.sum(running, axis=1, keepdims=True)
        return running / jnp.sum(running, axis=0, keepdims=True)

    return lax.fori_loop(0, BALANCE_ROUNDS, balance_round, grid)


def project_kernel(ids, *refs, counts, which, width):
    total = sum(sum(c) for c in counts)
    parts, (gain, w, out, gained, buf, sems) = list(refs[:total]), refs[total:]
    pieces = len(counts[0])
    copies = {}
    for k in range(pieces):
        for slot, third in enumerate(which):
            row = pl.multiple_of(ids[k] * width, width)
            copies[k, slot] = pltpu.make_async_copy(
                w.at[third, pl.ds(row, width), :],
                buf.at[slot, pl.ds(k * width, width), :],
                sems.at[slot * pieces + k],
            )
            copies[k, slot].start()
    starts = []
    for chunk in counts:
        starts.append(len(starts) and starts[-1] + sum(chunk_before))
        chunk_before = chunk
    height = gained.shape[0] // len(counts)
    squares = [None] * len(counts)
    accs = [None] * len(which)
    for k in range(pieces):
        span = slice(k * width, (k + 1) * width)
        g = gain[pl.ds(ids[k], 1), :]
        for i, chunk in enumerate(counts):
            row, sums = i * height, []
            begin = starts[i] + sum(chunk[:k])
            for part in parts[begin : begin + chunk[k]]:
                x = part[...].astype(f32)
                sums.append(jnp.sum(x * x, axis=1, keepdims=True))
                gained[row : row + part.shape[0], span] = (x * g).astype(bf16)
                row += part.shape[0]
            square = jnp.concatenate(sums, axis=0) if len(sums) > 1 else sums[0]
            squares[i] = square if k == 0 else squares[i] + square
        for slot in range(len(which)):
            copies[k, slot].wait()
            part = jnp.dot(gained[:, span], buf[slot, span], preferred_element_type=f32)
            accs[slot] = part if k == 0 else accs[slot] + part
    whole = jnp.concatenate(squares, axis=0) if len(squares) > 1 else squares[0]
    scale = lax.rsqrt(whole / (pieces * width) + norm_eps)
    for slot in range(len(which)):
        out[slot] = (accs[slot] * scale).astype(bf16)


def project(ids, chunks, gain, w3, which):
    pieces, width = gain.shape
    counts = [[len(piece) for piece in chunk] for chunk in chunks]
    parts = [part for chunk in chunks for piece in chunk for part in piece]
    m = sum(sum(part.shape[0] for part in chunk[0]) for chunk in chunks)
    full = lambda a: pl.BlockSpec(a.shape, lambda i, s: (0,) * a.ndim)
    return pl.pallas_call(
        functools.partial(project_kernel, counts=counts, which=which, width=width),
        grid_spec=pltpu.PrefetchScalarGridSpec(
            num_scalar_prefetch=1,
            grid=(1,),
            in_specs=[*map(full, parts), full(gain), pl.BlockSpec(memory_space=pl.ANY)],
            out_specs=pl.BlockSpec((len(which), m, width), lambda i, s: (0, 0, 0)),
            scratch_shapes=[
                pltpu.VMEM((m, pieces * width), bf16),
                pltpu.VMEM((len(which), pieces * width, width), bf16),
                pltpu.SemaphoreType.DMA((len(which) * pieces,)),
            ],
        ),
        out_shape=jax.ShapeDtypeStruct((len(which), m, width), bf16),
        compiler_params=pltpu.CompilerParams(vmem_limit_bytes=VMEM_LIMIT),
        cost_estimate=pl.CostEstimate(
            flops=2 * m * pieces * width * width * len(which),
            bytes_accessed=2 * pieces * width * width * len(which),
            transcendentals=0,
        ),
    )(ids, *parts, gain, w3)


def attend_kernel(q, marks, bases, *refs, spans, first, final, paired):
    kvs, refs = [], list(refs)
    for i in range(len(spans)):
        if paired:
            one, two = refs.pop(0), refs.pop(0)
            flag = bases[len(spans) + i] == 1
            kvs.append([jnp.where(flag, one[j], two[j]) for j in range(2)])
        else:
            kvs.append(refs.pop(0))
    if not first:
        ml_in, acc_in = refs[:2]
        refs = refs[2:]
    rows = q.shape[0]
    block = min(512, rows)
    factor = HEAD_DIM**-0.5 * math.log2(math.e)

    @pl.loop(0, rows // block)
    def _(b):
        cut = pl.ds(pl.multiple_of(b * block, block), block)
        queries = q[cut, :]
        start, pos = marks[0:1, cut], marks[1:2, cut]
        scores = []
        for i, (kv, causal) in enumerate(zip(kvs, spans)):
            s = lax.dot_general(
                kv[0], queries, (((1,), (1,)), ((), ())), preferred_element_type=f32
            )
            where = lax.broadcasted_iota(jnp.int32, s.shape, 0)
            allowed = where >= start - bases[i]
            if causal:
                allowed = allowed & (where <= pos - bases[i])
            scores.append(jnp.where(allowed, s, masked_score))
        top = functools.reduce(jnp.maximum, [jnp.max(s, axis=0, keepdims=True) for s in scores])
        if not first:
            old_top, old_sum = ml_in[0, 0:1, cut], ml_in[0, 1:2, cut]
            top = jnp.maximum(top, old_top)
        total, acc = None, None
        for s, kv in zip(scores, kvs):
            p = jnp.exp2((s - top) * factor)
            row = jnp.sum(p, axis=0, keepdims=True)
            part = lax.dot_general(
                kv[1], p.astype(bf16),
                (((0,), (0,)), ((), ())), preferred_element_type=f32,
            )
            total = row if total is None else total + row
            acc = part if acc is None else acc + part
        if not first:
            rescale = jnp.exp2((old_top - top) * factor)
            total = total + old_sum * rescale
            acc = acc + acc_in[0, :, cut] * rescale
        if final:
            refs[0][cut, :] = (acc / total).T.astype(bf16)
        else:
            ml_out, acc_out = refs
            ml_out[0, 0:1, cut] = top
            ml_out[0, 1:2, cut] = total
            acc_out[0, :, cut] = acc


def attend(q, marks, kvs, bases, spans, state, final):
    rows, width = q.shape
    heads = width // HEAD_DIM
    first = state is None
    paired = isinstance(kvs[0], tuple)
    if paired:
        kvs = [kv for pair in kvs for kv in pair]
    keys = sum(kv.shape[1] for kv in kvs)
    in_specs = [
        pl.BlockSpec((rows, HEAD_DIM), lambda h: (0, h)),
        pl.BlockSpec(marks.shape, lambda h: (0, 0)),
        pl.BlockSpec(memory_space=pltpu.SMEM),
    ]
    in_specs += [pl.BlockSpec((2, kv.shape[1], HEAD_DIM), lambda h: (0, 0, h)) for kv in kvs]
    operands = [q, marks, bases, *kvs]
    state_shapes = [(heads, 8, rows), (heads, HEAD_DIM, rows)]
    state_specs = [pl.BlockSpec((1,) + s[1:], lambda h: (h, 0, 0)) for s in state_shapes]
    aliases = {}
    if not first:
        if not final:
            aliases = {len(operands): 0, len(operands) + 1: 1}
        operands += list(state)
        in_specs += state_specs
    if final:
        out_specs = pl.BlockSpec((rows, HEAD_DIM), lambda h: (0, h))
        out_shape = jax.ShapeDtypeStruct((rows, width), bf16)
    else:
        out_specs = state_specs
        out_shape = [jax.ShapeDtypeStruct(s, f32) for s in state_shapes]
    return pl.pallas_call(
        functools.partial(attend_kernel, spans=spans, first=first, final=final, paired=paired),
        grid=(heads,),
        in_specs=in_specs,
        out_specs=out_specs,
        out_shape=out_shape,
        input_output_aliases=aliases,
        compiler_params=pltpu.CompilerParams(vmem_limit_bytes=VMEM_LIMIT),
        cost_estimate=pl.CostEstimate(
            flops=8 * rows * keys * width,
            bytes_accessed=8 * rows * width,
            transcendentals=heads * rows * keys,
        ),
    )(*operands)


def output_kernel(ids, context, w, *refs, half, kinds, count, columns):
    outs, (buf, sems) = refs[:-2], refs[-2:]
    copies = []
    for k in range(count):
        col = pl.multiple_of(ids[k] * columns, columns)
        copy = pltpu.make_async_copy(w.at[:, pl.ds(col, columns)], buf.at[k], sems.at[k])
        copy.start()
        copies.append(copy)
    for k in range(count):
        copies[k].wait()
        part = jnp.dot(context[...], buf[k], preferred_element_type=f32)
        if kinds is None:
            outs[0][k] = part.astype(bf16)
            continue
        for group, (out, slot) in enumerate(kinds[k]):
            piece = part[group * half : (group + 1) * half]
            outs[out][slot] = piece.astype(outs[out].dtype)


def output_projection(ids, context, chunk, rows, w_out, columns, pairwise):
    count = w_out.shape[1] // columns
    half = rows // 2
    kinds = None
    if pairwise:
        kinds = [
            [(1, 0), (3, 0)],
            [(0, 0), (3, 1)],
            [(1, 1), (2, 0)],
            [(0, 1), (2, 1)],
        ]
        out_shape = [
            jax.ShapeDtypeStruct((2, half, columns), dtype) for dtype in (bf16, f32, bf16, f32)
        ]
    else:
        out_shape = [jax.ShapeDtypeStruct((count, rows, columns), bf16)]
    out_specs = [pl.BlockSpec(s.shape, lambda i, s: (0, 0, 0)) for s in out_shape]
    return pl.pallas_call(
        functools.partial(output_kernel, half=half, kinds=kinds, count=count, columns=columns),
        grid_spec=pltpu.PrefetchScalarGridSpec(
            num_scalar_prefetch=1,
            grid=(1,),
            in_specs=[
                pl.BlockSpec((rows, context.shape[1]), lambda i, s: (chunk, 0)),
                pl.BlockSpec(memory_space=pl.ANY),
            ],
            out_specs=out_specs,
            scratch_shapes=[
                pltpu.VMEM((count, w_out.shape[0], columns), bf16),
                pltpu.SemaphoreType.DMA((count,)),
            ],
        ),
        out_shape=out_shape,
        compiler_params=pltpu.CompilerParams(vmem_limit_bytes=VMEM_LIMIT),
        cost_estimate=pl.CostEstimate(
            flops=2 * rows * w_out.size, bytes_accessed=2 * w_out.size, transcendentals=0
        ),
    )(ids, context, w_out)


def tie(value, *after):
    return lax.optimization_barrier((value, *after))[0]


def local(streams, doc_ids, mix_weight, mix_bias, attn_gain, w_qkv, w_out):
    n, n_streams, width = streams.shape
    tp = lax.axis_size("tp")
    seq = lax.axis_size("seq")
    model = width * tp
    shard = lax.axis_index("tp")
    seq_index = lax.axis_index("seq")
    core = seq_index % 2
    chip = seq_index // 2
    rows = 2 * n
    chunks = GATHER_CHUNKS
    m = n // chunks
    pairwise = tp == 4

    id_steps = gathered_ids(doc_ids)
    all_ids = id_steps[-1]
    most = max(0, (seq * n // 2 - rows) // m)

    def placed(all_ids):
        before = [jnp.sum((all_ids < d).astype(jnp.int32)) for d in range(DOCS)]

        def start_of(ids):
            start = jnp.full(ids.shape, before[0])
            for d in range(1, DOCS):
                start = jnp.where(ids >= d, before[d], start)
            return start

        marks = jnp.concatenate(
            [
                start_of(doc_ids)[None],
                (seq_index * n + jnp.arange(n, dtype=jnp.int32))[None],
                jnp.zeros((6, n), jnp.int32),
            ]
        )
        edges = jnp.arange(seq // 2, dtype=jnp.int32) * rows
        reach = jnp.max(edges - start_of(all_ids[::rows]))
        return marks, jnp.clip((reach - rows + m - 1) // m, 0, most)

    wide = streams.astype(f32)
    squares = jnp.sum(wide * wide, axis=(1, 2))
    next_wide = tie(streams, squares).astype(f32)
    logits = jnp.einsum("tsd,sdc->ct", next_wide, mix_weight, precision=lax.Precision.HIGHEST)
    summed = tp_sum(jnp.concatenate([logits, squares[None]], axis=0))
    root = jnp.sqrt(summed[-1] / (n_streams * model) + norm_eps)
    coef = summed[:-1] / root[None] + mix_bias[:, None]
    pre = jax.nn.sigmoid(coef[:n_streams])
    post = 2.0 * jax.nn.sigmoid(coef[n_streams : 2 * n_streams])
    raw = jnp.exp(coef[2 * n_streams :])
    pre_t = pre.T

    w3 = jnp.transpose(w_qkv, (1, 0, 2))
    gain = attn_gain.reshape(tp, width)
    if pairwise:
        ids = jnp.stack([shard ^ k for k in range(tp)])
    else:
        ids = jnp.arange(tp)
    mixed = [
        jnp.einsum(
            "ts,tsd->td", pre_t[c * m : (c + 1) * m], wide[c * m : (c + 1) * m],
            precision=lax.Precision.HIGHEST,
        ).astype(bf16)
        for c in range(chunks)
    ]
    raw = tie(raw, mixed[-1])
    mixing = doubly_stochastic(
        [[raw[i * n_streams + j] for j in range(n_streams)] for i in range(n_streams)]
    )
    pieces = []
    for c in range(chunks):
        if pairwise:
            from_x = by_xor(mixed[c], "tp", 1)
            from_y = by_xor(mixed[c], "tp", 2)
            pieces.append([[mixed[c]], [from_x], [from_y]])
        else:
            every = lax.all_gather(mixed[c], "tp", axis=0)
            pieces.append([[every[k]] for k in range(tp)])
    own_kv, other_kv, near_own, near_other = [], [], [], []
    for c in range(chunks):
        if pairwise:
            from_x, from_y = pieces[c][1][0], pieces[c][2][0]
            after = [*mixed[1:], id_steps[1]] if c == 0 else [own_kv[c - 1]]
            from_x, from_y = lax.optimization_barrier((from_x, from_y, *after))[:2]
            pieces[c].append([by_xor(from_y[: m // 2], "tp", 1), by_xor(from_x[m // 2 :], "tp", 2)])
        if c == 0:
            pieces[0][0][0] = tie(pieces[0][0][0], all_ids)
        elif c == 1:
            marks, level = placed(tie(all_ids, own_kv[0]))
            pieces[1][0][0] = tie(pieces[1][0][0], marks, level)
        kv = project(ids, [pieces[c]], gain, w3, (1, 2))
        own_kv.append(kv)
        near_own.append(next_chip(kv))
        other_kv.append(by_xor(kv, "seq", 1))
    q = project(ids, pieces, gain, w3, (0,))[0]
    early = chunks // 2
    for c in range(early):
        near_other.append(by_xor(tie(near_own[c], q), "seq", 1))

    def base_of(where, which, c):
        return where * rows + which * n + c * m

    def table(bases):
        return jnp.stack([jnp.asarray(b, jnp.int32) for b in bases])

    bases = [base_of(chip, core, c) for c in range(chunks)]
    bases += [jnp.where(core == 1, base_of(chip, 0, c), -(1 << 29)) for c in range(chunks)]
    bases += [base_of(chip - 1, which, c) for which in (core, 1 - core) for c in range(early)]
    state = attend(
        q, marks, own_kv + other_kv + near_own[:early] + near_other[:early], table(bases),
        [True] * chunks + [False] * (chunks + 2 * early), None, False,
    )
    for c in range(early, chunks):
        near_other.append(by_xor(tie(near_own[c], *state), "seq", 1))

    def finish(units, q, marks, state, near_own, near_other):
        late = near_own[early:] + near_other[early:]
        bases = [
            base_of(chip - 1, which, c) for which in (core, 1 - core) for c in range(early, chunks)
        ]
        if units == 0:
            return attend(q, marks, late, table(bases), [False] * len(late), state, True)
        held = {(which, c): near_own[c] for which in (0, 1) for c in range(chunks)}
        far, far_bases = [], []
        for u in range(units):
            hop, rest = 2 + u // (2 * chunks), u % (2 * chunks)
            which, c = 1 - rest // chunks, chunks - 1 - rest % chunks
            sent = lax.ppermute(
                held[which, c], "seq", [(i, i + 2) for i in range(which, seq - 2, 2)]
            )
            held[which, c] = sent
            far.append((which, sent))
            far_bases.append(base_of(chip - hop, which, c))
        state = attend(q, marks, late, table(bases), [False] * len(late), state, False)
        pairs = []
        for which, sent in far:
            shown = lax.ppermute(
                tie(sent, *state), "seq", [(i, i ^ 1) for i in range(which, seq, 2)]
            )
            pairs.append((sent, shown))
        far_bases += [(core == which).astype(jnp.int32) for which, _ in far]
        return attend(q, marks, pairs, table(far_bases), [False] * units, state, True)

    if most == 0:
        context = finish(0, q, marks, state, near_own, near_other)
    else:
        context = lax.switch(
            level,
            [functools.partial(finish, units) for units in range(most + 1)],
            q, marks, state, near_own, near_other,
        )

    r = n // SCATTER_CHUNKS
    firsts = []
    for c in range(SCATTER_CHUNKS):
        outs = output_projection(ids, context, c, r, w_out, width, pairwise)
        if pairwise:
            send_x, keep_x, send_y, keep_y = outs
            firsts.append(
                (
                    keep_x, by_xor(send_x, "tp", 1),
                    keep_y, by_xor(send_y, "tp", 2),
                )
            )
        else:
            firsts.append(lax.psum_scatter(outs[0], "tp", scatter_dimension=0, tiled=False))
    seconds = []
    for c in range(SCATTER_CHUNKS):
        if pairwise:
            keep_x, in_x, keep_y, in_y = firsts[c]
            next_y = (keep_x[1] + in_x[1].astype(f32)).astype(bf16)
            next_x = (keep_y[1] + in_y[1].astype(f32)).astype(bf16)
            seconds.append((by_xor(next_y, "tp", 2), by_xor(next_x, "tp", 1)))
    pieces = []
    for c in range(SCATTER_CHUNKS):
        if pairwise:
            keep_x, in_x, keep_y, in_y = firsts[c]
            end_y, end_x = seconds[c]
            pieces.append(keep_x[0] + in_x[0].astype(f32) + end_y.astype(f32))
            pieces.append(keep_y[0] + in_y[0].astype(f32) + end_x.astype(f32))
        else:
            pieces.append(firsts[c].astype(f32))
    branch = jnp.concatenate(pieces, axis=0)
    mix_t = jnp.transpose(mixing, (2, 0, 1))
    carried = jnp.einsum("tij,tjd->tid", mix_t, wide, precision=lax.Precision.HIGHEST)
    return (carried + post.T[:, :, None] * branch[:, None, :]).astype(bf16)


def solution(mesh):
    in_specs = (
        P("seq", None, "tp"),
        P("seq"),
        P(None, "tp", None),
        P(),
        P(),
        P(None, None, "tp"),
        P("tp", None),
    )

    return jax.shard_map(
        local, mesh=mesh, in_specs=in_specs, out_specs=P("seq", None, "tp"), check_vma=False
    )
```
